32 devices in a mesh: node: 2 (over x), tm: 4 (over z), space: 4 (over y, core).
Axes of the slice: x: 2, y: 2, z: 4, core: 2. Of those that a mesh axis runs over, the one named last changes fastest.
Arguments:
- nodes: float32 [4, 4, 32, 256, 256], P('tm', 'node', 'space'), may hold values from -1.5 to 1.5
- prev_final: float32 [4, 32, 256, 256], P('tm', 'space'), may hold values from -6 to 6
- u_init: float32 [32, 256, 256], P('space'), may hold values from -6 to 6
- conductivity: float32 [32, 256, 256], P('space'), may hold values from 0.25 to 16
Outputs:
- new_nodes: float32 [4, 4, 32, 256, 256], P('tm', 'node', 'space')
The draws below stay inside these ranges and needn't reach their ends.
All inputs are finite; a program needn't handle non-finite values.
Results may differ from the reference program's by a relative error of at most 0.0003.
Values sent between devices are 32-bit elements; how exact they have to be, the bound alone decides.
A program may use at most 128 MiB of HBM per device.

```python
import jax
import jax.numpy as jnp
from jax import lax

NY = 256
NZ = 256
NODES = 4
SWEEPS = 8
BLOCKS = 4
NX = 32


def draw_nodes(key, part):
    full_shape = (BLOCKS, NODES, NX, NY, NZ)
    x_index = lax.broadcasted_iota(jnp.int32, full_shape, 2)
    y_index = lax.broadcasted_iota(jnp.int32, full_shape, 3)
    z_index = lax.broadcasted_iota(jnp.int32, full_shape, 4)
    parity_sign = (1 - 2 * ((x_index + y_index + z_index) % 2)).astype(jnp.float32)
    magnitude = 1.0 + 0.25 * jnp.clip(jax.random.normal(key, full_shape, jnp.float32), -2.0, 2.0)
    return parity_sign * magnitude


def draw_conductivity(key, part):
    full_shape = (NX, NY, NZ)
    y_index = lax.broadcasted_iota(jnp.int32, full_shape, 1)
    z_index = lax.broadcasted_iota(jnp.int32, full_shape, 2)
    channel = (y_index + z_index) % 2 == 0
    key_high = jax.random.fold_in(key, 11)
    key_low = jax.random.fold_in(key, 23)
    high_values = 8.0 * jnp.exp(0.6931472 * jax.random.uniform(key_high, full_shape, jnp.float32, 0.0, 1.0))
    low_values = 0.25 * jnp.exp(0.6931472 * jax.random.uniform(key_low, full_shape, jnp.float32, 0.0, 1.0))
    return jnp.clip(jnp.where(channel, high_values, low_values), 0.25, 16.0)


def steps_of(key, shape, shards, least, high):
    def one(axis_at, parts):
        steps = jax.random.uniform(jax.random.fold_in(jax.random.fold_in(key, 6), axis_at), (parts,), jnp.float32, least / len(shards), high / len(shards))
        return jnp.repeat(jnp.exp(steps), shape[axis_at] // parts).reshape((-1,) + (1,) * (len(shape) - axis_at - 1))

    factor_of = one(*shards[0])
    for cut in shards[1:]:
        factor_of = factor_of * one(*cut)
    return factor_of


def centred(own_key, dims, scale, reach, pieces=(), dtype=jnp.bfloat16):
    values = scale * jax.random.normal(own_key, dims, jnp.float32)
    if pieces:
        values = values * steps_of(own_key, dims, pieces, -0.22, 0.18)
    return jnp.clip(values, -reach, reach).astype(dtype)


def setup_inputs(seed: int = 0) -> dict:
    arg_keys = jax.random.split(jax.random.key(seed), 5)
    nodes = draw_nodes(jax.random.fold_in(arg_keys[4], 71), 0)
    prev_final = centred(arg_keys[1], (BLOCKS, NX, NY, NZ), 1.0, 6.0, ((0, 4), (1, 4)), jnp.float32)
    u_init = centred(arg_keys[2], (NX, NY, NZ), 1.0, 6.0, ((0, 4),), jnp.float32)
    conductivity = draw_conductivity(jax.random.fold_in(arg_keys[4], 71), 0)
    return {"nodes": nodes, "prev_final": prev_final, "u_init": u_init, "conductivity": conductivity}


radau_points = [0.08858795951270394, 0.40946686444073470, 0.78765946176084705, 1.0]


def mixing_table():
    count_nodes = len(radau_points)
    table = [[0.0] * count_nodes for row_index in range(count_nodes)]
    for column in range(count_nodes):
        coefs = [1.0]
        for other in range(count_nodes):
            if other != column:
                scale = 1.0 / (radau_points[column] - radau_points[other])
                shifted = [0.0] + coefs
                lowered = [value * radau_points[other] for value in coefs] + [0.0]
                coefs = [(shifted[k] - lowered[k]) * scale for k in range(len(shifted))]
        for row_index in range(count_nodes):
            point = radau_points[row_index]
            integral = 0.0
            for power in range(len(coefs)):
                integral = integral + coefs[power] * point ** (power + 1) / (power + 1)
            table[row_index][column] = integral
        table[column][column] = table[column][column] - radau_points[column]
    return table


def from_lower(values, axis):
    axis = axis % values.ndim
    widths = [(0, 0)] * values.ndim
    widths[axis] = (1, 0)
    return lax.slice_in_dim(jnp.pad(values, widths), 0, values.shape[axis], axis=axis)


def from_upper(values, axis):
    axis = axis % values.ndim
    widths = [(0, 0)] * values.ndim
    widths[axis] = (0, 1)
    return lax.slice_in_dim(jnp.pad(values, widths), 1, values.shape[axis] + 1, axis=axis)


def coefficients(conduct_ext):
    centre = conduct_ext[1:-1]
    face_xl = 0.5 * (centre + conduct_ext[:-2])
    face_xr = 0.5 * (centre + conduct_ext[2:])
    padded_y = jnp.pad(centre, ((0, 0), (1, 1), (0, 0)), mode="edge")
    face_yl = 0.5 * (centre + padded_y[:, :-2])
    face_yr = 0.5 * (centre + padded_y[:, 2:])
    padded_z = jnp.pad(centre, ((0, 0), (0, 0), (1, 1)), mode="edge")
    face_zl = 0.5 * (centre + padded_z[:, :, :-2])
    face_zr = 0.5 * (centre + padded_z[:, :, 2:])
    summed = face_xl + face_xr + face_yl + face_yr + face_zl + face_zr
    return (face_xl, face_xr, face_yl, face_yr, face_zl, face_zr, summed)


def neighbours(padded, faces):
    centre = padded[..., 1:-1, :, :]
    result = faces[0] * padded[..., :-2, :, :] + faces[1] * padded[..., 2:, :, :]
    result = result + faces[2] * from_lower(centre, -2) + faces[3] * from_upper(centre, -2)
    result = result + faces[4] * from_lower(centre, -1) + faces[5] * from_upper(centre, -1)
    return result


def reference(nodes, prev_final, u_init, conductivity):
    faces = coefficients(jnp.pad(conductivity, ((1, 1), (0, 0), (0, 0)), mode="edge"))
    weights = jnp.asarray(mixing_table(), jnp.float32)
    node_diag = jnp.asarray(radau_points, jnp.float32)[:, None, None, None]
    starts = jnp.concatenate([u_init[None], prev_final[:-1]], axis=0)
    divisor = 1.0 + node_diag * faces[6]

    def block(pair):
        current, block_start = pair
        padded = jnp.pad(current, ((0, 0), (1, 1), (0, 0), (0, 0)))
        fluxes = neighbours(padded, faces) - faces[6] * current
        right_side = block_start[None] + jnp.einsum("mj,jxyz->mxyz", weights, fluxes, precision=lax.Precision.HIGHEST)
        iterate = current
        for repeat_index in range(SWEEPS):
            padded = jnp.pad(iterate, ((0, 0), (1, 1), (0, 0), (0, 0)))
            iterate = (right_side + node_diag * neighbours(padded, faces)) / divisor
        return iterate

    return lax.map(block, (nodes, starts))
```

```python
import functools

import jax
import jax.numpy as jnp
from jax import lax
from jax.experimental import pallas as pl
from jax.experimental.pallas import tpu as pltpu
from jax.sharding import PartitionSpec as P

SWEEPS = 8
ROWS = 16
PAD = 8
MESH = pl.DeviceIdType.MESH

radau_points = [0.08858795951270394, 0.4094668644407347, 0.787659461760847, 1.0]


def mixing_table():
    count_nodes = len(radau_points)
    table = [[0.0] * count_nodes for row_index in range(count_nodes)]
    for column in range(count_nodes):
        coefs = [1.0]
        for other in range(count_nodes):
            if other != column:
                scale = 1.0 / (radau_points[column] - radau_points[other])
                shifted = [0.0] + coefs
                lowered = [value * radau_points[other] for value in coefs] + [0.0]
                coefs = [(shifted[k] - lowered[k]) * scale for k in range(len(shifted))]
        for row_index in range(count_nodes):
            point = radau_points[row_index]
            integral = 0.0
            for power in range(len(coefs)):
                integral = integral + coefs[power] * point ** (power + 1) / (power + 1)
            table[row_index][column] = integral
        table[column][column] = table[column][column] - radau_points[column]
    return table


def pick(position, values):
    result = jnp.float32(values[0])
    for k in range(1, len(values)):
        result = jnp.where(position == k, jnp.float32(values[k]), result)
    return result


def kernel(
    sizes, nodes, prev, init, cond, out,
    own, theirs, start, even, odd, kpad, fx, fyl, fyr, fzl, fzr, inv, rhs, result,
    load_sem, k_send, k_recv, node_send, node_recv, prev_send, prev_recv,
    halo_send, halo_recv, out_sem,
):
    n_node, n_tm, n_space, per, bricks, height = sizes
    chunks = height // ROWS
    node = lax.axis_index("node")
    tm = lax.axis_index("tm")
    space = lax.axis_index("space")
    has_lower = space > 0
    has_upper = space < n_space - 1
    lower = jnp.maximum(space - 1, 0)
    upper = jnp.minimum(space + 1, n_space - 1)
    later = jnp.minimum(tm + 1, n_tm - 1)
    earlier = jnp.maximum(tm - 1, 0)
    first_tm = tm == 0
    last_tm = tm == n_tm - 1
    inner = pl.ds(PAD, height)

    table = mixing_table()
    mix = [
        [
            [
                pick(
                    node,
                    [
                        table[p * per + i][((p + n_node - d) % n_node) * per + j]
                        / radau_points[p * per + i]
                        for p in range(n_node)
                    ],
                )
                for j in range(per)
            ]
            for d in range(n_node)
        ]
        for i in range(per)
    ]
    point = [pick(node, [radau_points[p * per + i] for p in range(n_node)]) for i in range(per)]
    inv_point = [pick(node, [1.0 / radau_points[p * per + i] for p in range(n_node)]) for i in range(per)]

    def k_up():
        return pltpu.make_async_remote_copy(
            cond.at[bricks - 1], kpad.at[0, inner], k_send.at[0], k_recv.at[0],
            device_id={"space": upper}, device_id_type=MESH)

    def k_down():
        return pltpu.make_async_remote_copy(
            cond.at[0], kpad.at[bricks + 1, inner], k_send.at[1], k_recv.at[1],
            device_id={"space": lower}, device_id_type=MESH)

    def k_edge_low():
        return pltpu.make_async_copy(cond.at[0], kpad.at[0, inner], k_recv.at[0])

    def k_edge_high():
        return pltpu.make_async_copy(cond.at[bricks - 1], kpad.at[bricks + 1, inner], k_recv.at[1])

    def node_copy(d, b):
        rows = pl.ds(pl.multiple_of(b * ROWS, ROWS), ROWS)
        return pltpu.make_async_remote_copy(
            nodes.at[0, :, :, rows], theirs.at[d - 1, :, :, rows],
            node_send.at[d - 1, b], node_recv.at[d - 1, b],
            device_id={"node": lax.rem(node + d, n_node)}, device_id_type=MESH)

    def prev_copy(b):
        rows = pl.ds(pl.multiple_of(b * ROWS, ROWS), ROWS)
        return pltpu.make_async_remote_copy(
            prev.at[0, :, rows], start.at[:, rows], prev_send.at[b], prev_recv.at[b],
            device_id={"tm": later}, device_id_type=MESH)

    def init_copy(b):
        rows = pl.ds(pl.multiple_of(b * ROWS, ROWS), ROWS)
        return pltpu.make_async_copy(init.at[:, rows], start.at[:, rows], prev_recv.at[b])

    def halo_up(buffer, s, b):
        rows = pl.ds(pl.multiple_of(PAD + b * ROWS, 8), ROWS)
        return pltpu.make_async_remote_copy(
            buffer.at[:, bricks, rows], buffer.at[:, 0, rows],
            halo_send.at[0, s], halo_recv.at[0, s, b],
            device_id={"space": upper}, device_id_type=MESH)

    def halo_down(buffer, s, b):
        rows = pl.ds(pl.multiple_of(PAD + b * ROWS, 8), ROWS)
        return pltpu.make_async_remote_copy(
            buffer.at[:, 1, rows], buffer.at[:, bricks + 1, rows],
            halo_send.at[1, s], halo_recv.at[1, s, b],
            device_id={"space": lower}, device_id_type=MESH)

    def out_copy(b):
        rows = pl.ds(pl.multiple_of(b * ROWS, ROWS), ROWS)
        return pltpu.make_async_copy(result.at[:, :, rows], out.at[0, :, :, rows], out_sem.at[b])

    own_load = pltpu.make_async_copy(nodes.at[0], own, load_sem.at[0])
    k_load = pltpu.make_async_copy(cond, kpad.at[pl.ds(1, bricks), inner], load_sem.at[1])
    own_load.start()
    k_load.start()

    barrier = pltpu.get_barrier_semaphore()
    partners = [(None, {"node": lax.rem(node + d, n_node)}) for d in range(1, n_node)]
    if n_space > 1:
        partners += [(has_lower, {"space": lower}), (has_upper, {"space": upper})]
    if n_tm > 1:
        partners += [(jnp.logical_not(first_tm), {"tm": earlier}), (jnp.logical_not(last_tm), {"tm": later})]
    for guard, target in partners:
        def greet(target=target):
            pl.semaphore_signal(barrier, inc=1, device_id=target, device_id_type=MESH)
        greet() if guard is None else pl.when(guard)(greet)
    peers = n_node - 1
    if n_space > 1:
        peers = peers + has_lower.astype(jnp.int32) + has_upper.astype(jnp.int32)
    if n_tm > 1:
        peers = peers + (tm > 0).astype(jnp.int32) + (tm < n_tm - 1).astype(jnp.int32)
    pl.semaphore_wait(barrier, peers)

    if n_space > 1:
        pl.when(has_upper)(lambda: k_up().start())
        pl.when(has_lower)(lambda: k_down().start())
    pl.when(jnp.logical_not(has_lower))(lambda: k_edge_low().start())
    pl.when(jnp.logical_not(has_upper))(lambda: k_edge_high().start())

    @pl.loop(0, chunks)
    def _(b):
        for d in range(1, n_node):
            node_copy(d, b).start()
        if n_tm > 1:
            pl.when(jnp.logical_not(last_tm))(lambda: prev_copy(b).start())
        pl.when(first_tm)(lambda: init_copy(b).start())

    width = even.shape[-1]
    for buffer in (even, odd):
        for i in range(per):
            for x in range(bricks + 2):
                buffer[i, x, pl.ds(0, PAD)] = jnp.zeros((PAD, width), jnp.float32)
                buffer[i, x, pl.ds(PAD + height, PAD)] = jnp.zeros((PAD, width), jnp.float32)

        @pl.when(jnp.logical_not(has_lower))
        def _():
            @pl.loop(0, chunks)
            def _(b):
                rows = pl.ds(pl.multiple_of(PAD + b * ROWS, 8), ROWS)
                for i in range(per):
                    buffer[i, 0, rows] = jnp.zeros((ROWS, width), jnp.float32)

        @pl.when(jnp.logical_not(has_upper))
        def _():
            @pl.loop(0, chunks)
            def _(b):
                rows = pl.ds(pl.multiple_of(PAD + b * ROWS, 8), ROWS)
                for i in range(per):
                    buffer[i, bricks + 1, rows] = jnp.zeros((ROWS, width), jnp.float32)

    k_load.wait()
    if n_space > 1:
        pl.when(has_lower)(lambda: k_up().wait_recv())
        pl.when(has_upper)(lambda: k_down().wait_recv())
    pl.when(jnp.logical_not(has_lower))(lambda: k_edge_low().wait())
    pl.when(jnp.logical_not(has_upper))(lambda: k_edge_high().wait())
    for x in range(bricks + 2):
        kpad[x, pl.ds(0, PAD)] = jnp.broadcast_to(kpad[x, pl.ds(PAD, 1)], (PAD, width))
        kpad[x, pl.ds(PAD + height, PAD)] = jnp.broadcast_to(kpad[x, pl.ds(PAD + height - 1, 1)], (PAD, width))
    own_load.wait()

    def first_stage(b):
        r = pl.multiple_of(b * ROWS, ROWS)
        rows = pl.ds(r, ROWS)
        inside = pl.ds(pl.multiple_of(r + PAD, 8), ROWS)
        column = lax.broadcasted_iota(jnp.int32, (ROWS, width), 1)
        at_first = column == 0
        at_last = column == width - 1
        for x in range(bricks):
            window = kpad[x + 1, pl.ds(r, ROWS + 2 * PAD)]
            k = window[PAD : PAD + ROWS]
            xl = 0.5 * (k + kpad[x, inside])
            xr = 0.5 * (k + kpad[x + 2, inside])
            yl = 0.5 * (k + window[PAD - 1 : PAD - 1 + ROWS])
            yr = 0.5 * (k + window[PAD + 1 : PAD + 1 + ROWS])
            zl = 0.5 * (k + jnp.where(at_first, k, pltpu.roll(k, 1, 1)))
            zr = 0.5 * (k + jnp.where(at_last, k, pltpu.roll(k, width - 1, 1)))
            total = xl + xr + yl + yr + zl + zr
            fx[x, rows] = xl
            if x == bricks - 1:
                fx[bricks, rows] = xr
            fyl[x, rows] = yl
            fyr[x, rows] = yr
            fzl[x, rows] = jnp.where(at_first, 0.0, zl)
            fzr[x, rows] = jnp.where(at_last, 0.0, zr)
            for i in range(per):
                inv[i, x, rows] = 1.0 / (inv_point[i] + total)
        for d in range(1, n_node):
            node_copy(d, b).wait_recv()
        pl.when(first_tm)(lambda: init_copy(b).wait())
        if n_tm > 1:
            pl.when(jnp.logical_not(first_tm))(lambda: prev_copy(b).wait_recv())
        for x in range(bricks):
            mine = [own[j, x, rows] for j in range(per)]
            states = [mine] + [[theirs[d - 1, j, x, rows] for j in range(per)] for d in range(1, n_node)]
            begin = start[x, rows]
            for i in range(per):
                q = mix[i][0][0] * states[0][0]
                for d in range(n_node):
                    for j in range(per):
                        if d or j:
                            q = q + mix[i][d][j] * states[d][j]
                even[i, x + 1, inside] = mine[i] + q
                rhs[i, x, rows] = (begin + q) * inv_point[i]

    def sweep(src, dst, b, last):
        r = pl.multiple_of(b * ROWS, ROWS)
        rows = pl.ds(r, ROWS)
        inside = pl.ds(pl.multiple_of(r + PAD, 8), ROWS)
        for x in range(bricks):
            xl, xr = fx[x, rows], fx[x + 1, rows]
            yl, yr = fyl[x, rows], fyr[x, rows]
            zl, zr = fzl[x, rows], fzr[x, rows]
            for i in range(per):
                window = src[i, x + 1, pl.ds(r, ROWS + 2 * PAD)]
                centre = window[PAD : PAD + ROWS]
                right = rhs[i, x, rows]
                value = xl * src[i, x, inside] + xr * src[i, x + 2, inside]
                value = value + yl * window[PAD - 1 : PAD - 1 + ROWS]
                value = value + yr * window[PAD + 1 : PAD + 1 + ROWS]
                value = value + zl * pltpu.roll(centre, 1, 1)
                value = value + zr * pltpu.roll(centre, width - 1, 1)
                value = (value + right) * inv[i, x, rows]
                if last:
                    result[i, x, rows] = value - (point[i] * right - start[x, rows])
                else:
                    dst[i, x + 1, inside] = value

    def receive(buffer, s, b):
        if n_space > 1:
            pl.when(has_lower)(lambda: halo_up(buffer, s, b).wait_recv())
            pl.when(has_upper)(lambda: halo_down(buffer, s, b).wait_recv())

    def send(buffer, s, b):
        if n_space > 1:
            @pl.when(has_upper)
            def _():
                pl.when(b > 0)(lambda: halo_up(buffer, s, b - 1).wait_send())
                halo_up(buffer, s, b).start()

            @pl.when(has_lower)
            def _():
                pl.when(b > 0)(lambda: halo_down(buffer, s, b - 1).wait_send())
                halo_down(buffer, s, b).start()

    def settle(buffer, s):
        if n_space > 1:
            pl.when(has_upper)(lambda: halo_up(buffer, s, chunks - 1).wait_send())
            pl.when(has_lower)(lambda: halo_down(buffer, s, chunks - 1).wait_send())

    def stage(src, dst, s, t, last=False):
        b = t - 2 * s

        @pl.when((b >= 0) & (b < chunks))
        def _():
            receive(src, s - 1, b)
            sweep(src, dst, b, last)
            if last:
                out_copy(b).start()
            else:
                send(dst, s, b)

        if not last:
            pl.when(b == chunks)(lambda: settle(dst, s))

    pairs = SWEEPS // 2

    @pl.loop(0, chunks + 2 * SWEEPS)
    def _(t):
        stage(odd, None, SWEEPS, t, last=True)
        stage(even, odd, SWEEPS - 1, t)

        @pl.loop(0, pairs - 1)
        def _(j):
            stage(odd, even, SWEEPS - 2 - 2 * j, t)
            stage(even, odd, SWEEPS - 3 - 2 * j, t)

        @pl.when(t < chunks)
        def _():
            first_stage(t)
            send(even, 0, t)

        pl.when(t == chunks)(lambda: settle(even, 0))

    if n_space > 1:
        pl.when(has_upper)(lambda: k_up().wait_send())
        pl.when(has_lower)(lambda: k_down().wait_send())

    @pl.loop(0, chunks)
    def _(b):
        for d in range(1, n_node):
            node_copy(d, b).wait_send()
        if n_tm > 1:
            pl.when(jnp.logical_not(last_tm))(lambda: prev_copy(b).wait_send())
        out_copy(b).wait()


def body(n_node, n_tm, n_space, nodes, prev_final, u_init, conductivity):
    per, bricks, height, width = nodes.shape[1:]
    chunks = height // ROWS
    field = (bricks, height, width)
    f32 = jnp.float32
    vmem = pltpu.VMEM
    dma = pltpu.SemaphoreType.DMA
    others = max(n_node - 1, 1)
    return pl.pallas_call(
        functools.partial(kernel, (n_node, n_tm, n_space, per, bricks, height)),
        out_shape=jax.ShapeDtypeStruct(nodes.shape, f32),
        in_specs=[pl.BlockSpec(memory_space=pl.ANY)] * 4,
        out_specs=pl.BlockSpec(memory_space=pl.ANY),
        scratch_shapes=[
            vmem((per,) + field, f32),
            vmem((others, per) + field, f32),
            vmem(field, f32),
            vmem((per, bricks + 2, height + 2 * PAD, width), f32),
            vmem((per, bricks + 2, height + 2 * PAD, width), f32),
            vmem((bricks + 2, height + 2 * PAD, width), f32),
            vmem((bricks + 1, height, width), f32),
            vmem(field, f32),
            vmem(field, f32),
            vmem(field, f32),
            vmem(field, f32),
            vmem((per,) + field, f32),
            vmem((per,) + field, f32),
            vmem((per,) + field, f32),
            dma((2,)),
            dma((2,)),
            dma((2,)),
            dma((others, chunks)),
            dma((others, chunks)),
            dma((chunks,)),
            dma((chunks,)),
            dma((2, SWEEPS)),
            dma((2, SWEEPS, chunks)),
            dma((chunks,)),
        ],
        compiler_params=pltpu.CompilerParams(
            collective_id=0, has_side_effects=True, vmem_limit_bytes=58 * 1024 * 1024
        ),
        name="sdc_sweep",
    )(nodes, prev_final, u_init, conductivity)


def solution(mesh):
    in_specs = (
        P("tm", "node", "space", None, None),
        P("tm", "space", None, None),
        P("space", None, None),
        P("space", None, None),
    )
    out_specs = P("tm", "node", "space", None, None)
    sized = functools.partial(body, mesh.shape["node"], mesh.shape["tm"], mesh.shape["space"])
    return jax.shard_map(sized, mesh=mesh, in_specs=in_specs, out_specs=out_specs, check_vma=False)
```

```python
import functools

import jax
import jax.numpy as jnp
from jax import lax
from jax.experimental import pallas as pl
from jax.experimental.pallas import tpu as pltpu
from jax.sharding import PartitionSpec as P

SWEEPS = 8
ROWS = 16
PAD = 8
MESH = pl.DeviceIdType.MESH

radau_points = [0.08858795951270394, 0.4094668644407347, 0.787659461760847, 1.0]


def mixing_table():
    count_nodes = len(radau_points)
    table = [[0.0] * count_nodes for row_index in range(count_nodes)]
    for column in range(count_nodes):
        coefs = [1.0]
        for other in range(count_nodes):
            if other != column:
                scale = 1.0 / (radau_points[column] - radau_points[other])
                shifted = [0.0] + coefs
                lowered = [value * radau_points[other] for value in coefs] + [0.0]
                coefs = [(shifted[k] - lowered[k]) * scale for k in range(len(shifted))]
        for row_index in range(count_nodes):
            point = radau_points[row_index]
            integral = 0.0
            for power in range(len(coefs)):
                integral = integral + coefs[power] * point ** (power + 1) / (power + 1)
            table[row_index][column] = integral
        table[column][column] = table[column][column] - radau_points[column]
    return table


def pick(position, values):
    result = jnp.float32(values[0])
    for k in range(1, len(values)):
        result = jnp.where(position == k, jnp.float32(values[k]), result)
    return result


def kernel(
    sizes, nodes, prev, init, cond, out,
    own, theirs, start, even, odd, kpad, fx, fyl, fyr, fzl, fzr, inv, rhs,
    load_sem, k_send, k_recv, node_send, node_recv, prev_send, prev_recv,
    halo_send, halo_recv,
):
    n_node, n_tm, n_space, per, bricks, height = sizes
    chunks = height // ROWS
    node = lax.axis_index("node")
    tm = lax.axis_index("tm")
    space = lax.axis_index("space")
    has_lower = space > 0
    has_upper = space < n_space - 1
    lower = jnp.maximum(space - 1, 0)
    upper = jnp.minimum(space + 1, n_space - 1)
    later = jnp.minimum(tm + 1, n_tm - 1)
    earlier = jnp.maximum(tm - 1, 0)
    first_tm = tm == 0
    last_tm = tm == n_tm - 1
    inner = pl.ds(PAD, height)

    table = mixing_table()
    mix = [
        [
            [
                pick(
                    node,
                    [
                        table[p * per + i][((p + n_node - d) % n_node) * per + j]
                        / radau_points[p * per + i]
                        for p in range(n_node)
                    ],
                )
                for j in range(per)
            ]
            for d in range(n_node)
        ]
        for i in range(per)
    ]
    point = [pick(node, [radau_points[p * per + i] for p in range(n_node)]) for i in range(per)]
    inv_point = [pick(node, [1.0 / radau_points[p * per + i] for p in range(n_node)]) for i in range(per)]

    def k_up():
        return pltpu.make_async_remote_copy(
            cond.at[bricks - 1], kpad.at[0, inner], k_send.at[0], k_recv.at[0],
            device_id={"space": upper}, device_id_type=MESH)

    def k_down():
        return pltpu.make_async_remote_copy(
            cond.at[0], kpad.at[bricks + 1, inner], k_send.at[1], k_recv.at[1],
            device_id={"space": lower}, device_id_type=MESH)

    def k_edge_low():
        return pltpu.make_async_copy(cond.at[0], kpad.at[0, inner], k_recv.at[0])

    def k_edge_high():
        return pltpu.make_async_copy(cond.at[bricks - 1], kpad.at[bricks + 1, inner], k_recv.at[1])

    def node_copy(d, b):
        rows = pl.ds(pl.multiple_of(b * ROWS, ROWS), ROWS)
        return pltpu.make_async_remote_copy(
            nodes.at[0, :, :, rows], theirs.at[d - 1, :, :, rows],
            node_send.at[d - 1, b], node_recv.at[d - 1, b],
            device_id={"node": lax.rem(node + d, n_node)}, device_id_type=MESH)

    def prev_copy(b):
        rows = pl.ds(pl.multiple_of(b * ROWS, ROWS), ROWS)
        return pltpu.make_async_remote_copy(
            prev.at[0, :, rows], start.at[:, rows], prev_send.at[b], prev_recv.at[b],
            device_id={"tm": later}, device_id_type=MESH)

    def init_copy(b):
        rows = pl.ds(pl.multiple_of(b * ROWS, ROWS), ROWS)
        return pltpu.make_async_copy(init.at[:, rows], start.at[:, rows], prev_recv.at[b])

    def halo_up(buffer, s, b):
        rows = pl.ds(pl.multiple_of(PAD + b * ROWS, 8), ROWS)
        return pltpu.make_async_remote_copy(
            buffer.at[:, bricks, rows], buffer.at[:, 0, rows],
            halo_send.at[0, s], halo_recv.at[0, s, b],
            device_id={"space": upper}, device_id_type=MESH)

    def halo_down(buffer, s, b):
        rows = pl.ds(pl.multiple_of(PAD + b * ROWS, 8), ROWS)
        return pltpu.make_async_remote_copy(
            buffer.at[:, 1, rows], buffer.at[:, bricks + 1, rows],
            halo_send.at[1, s], halo_recv.at[1, s, b],
            device_id={"space": lower}, device_id_type=MESH)

    own_load = pltpu.make_async_copy(nodes.at[0], own, load_sem.at[0])
    k_load = pltpu.make_async_copy(cond, kpad.at[pl.ds(1, bricks), inner], load_sem.at[1])
    own_load.start()
    k_load.start()

    barrier = pltpu.get_barrier_semaphore()
    partners = [(None, {"node": lax.rem(node + d, n_node)}) for d in range(1, n_node)]
    if n_space > 1:
        partners += [(has_lower, {"space": lower}), (has_upper, {"space": upper})]
    if n_tm > 1:
        partners += [(jnp.logical_not(first_tm), {"tm": earlier}), (jnp.logical_not(last_tm), {"tm": later})]
    for guard, target in partners:
        def greet(target=target):
            pl.semaphore_signal(barrier, inc=1, device_id=target, device_id_type=MESH)
        greet() if guard is None else pl.when(guard)(greet)
    peers = n_node - 1
    if n_space > 1:
        peers = peers + has_lower.astype(jnp.int32) + has_upper.astype(jnp.int32)
    if n_tm > 1:
        peers = peers + (tm > 0).astype(jnp.int32) + (tm < n_tm - 1).astype(jnp.int32)
    pl.semaphore_wait(barrier, peers)

    if n_space > 1:
        pl.when(has_upper)(lambda: k_up().start())
        pl.when(has_lower)(lambda: k_down().start())
    pl.when(jnp.logical_not(has_lower))(lambda: k_edge_low().start())
    pl.when(jnp.logical_not(has_upper))(lambda: k_edge_high().start())

    @pl.loop(0, chunks)
    def _(b):
        for d in range(1, n_node):
            node_copy(d, b).start()
        if n_tm > 1:
            pl.when(jnp.logical_not(last_tm))(lambda: prev_copy(b).start())
        pl.when(first_tm)(lambda: init_copy(b).start())

    width = even.shape[-1]
    for buffer in (even, odd):
        for i in range(per):
            for x in range(bricks + 2):
                buffer[i, x, pl.ds(0, PAD)] = jnp.zeros((PAD, width), jnp.float32)
                buffer[i, x, pl.ds(PAD + height, PAD)] = jnp.zeros((PAD, width), jnp.float32)

        @pl.when(jnp.logical_not(has_lower))
        def _():
            @pl.loop(0, chunks)
            def _(b):
                rows = pl.ds(pl.multiple_of(PAD + b * ROWS, 8), ROWS)
                for i in range(per):
                    buffer[i, 0, rows] = jnp.zeros((ROWS, width), jnp.float32)

        @pl.when(jnp.logical_not(has_upper))
        def _():
            @pl.loop(0, chunks)
            def _(b):
                rows = pl.ds(pl.multiple_of(PAD + b * ROWS, 8), ROWS)
                for i in range(per):
                    buffer[i, bricks + 1, rows] = jnp.zeros((ROWS, width), jnp.float32)

    k_load.wait()
    if n_space > 1:
        pl.when(has_lower)(lambda: k_up().wait_recv())
        pl.when(has_upper)(lambda: k_down().wait_recv())
    pl.when(jnp.logical_not(has_lower))(lambda: k_edge_low().wait())
    pl.when(jnp.logical_not(has_upper))(lambda: k_edge_high().wait())
    for x in range(bricks + 2):
        kpad[x, pl.ds(0, PAD)] = jnp.broadcast_to(kpad[x, pl.ds(PAD, 1)], (PAD, width))
        kpad[x, pl.ds(PAD + height, PAD)] = jnp.broadcast_to(kpad[x, pl.ds(PAD + height - 1, 1)], (PAD, width))
    own_load.wait()

    def first_stage(b):
        r = pl.multiple_of(b * ROWS, ROWS)
        rows = pl.ds(r, ROWS)
        inside = pl.ds(pl.multiple_of(r + PAD, 8), ROWS)
        column = lax.broadcasted_iota(jnp.int32, (ROWS, width), 1)
        at_first = column == 0
        at_last = column == width - 1
        for x in range(bricks):
            window = kpad[x + 1, pl.ds(r, ROWS + 2 * PAD)]
            k = window[PAD : PAD + ROWS]
            xl = 0.5 * (k + kpad[x, inside])
            xr = 0.5 * (k + kpad[x + 2, inside])
            yl = 0.5 * (k + window[PAD - 1 : PAD - 1 + ROWS])
            yr = 0.5 * (k + window[PAD + 1 : PAD + 1 + ROWS])
            zl = 0.5 * (k + jnp.where(at_first, k, pltpu.roll(k, 1, 1)))
            zr = 0.5 * (k + jnp.where(at_last, k, pltpu.roll(k, width - 1, 1)))
            total = xl + xr + yl + yr + zl + zr
            fx[x, rows] = xl
            if x == bricks - 1:
                fx[bricks, rows] = xr
            fyl[x, rows] = yl
            fyr[x, rows] = yr
            fzl[x, rows] = jnp.where(at_first, 0.0, zl)
            fzr[x, rows] = jnp.where(at_last, 0.0, zr)
            for i in range(per):
                inv[i, x, rows] = 1.0 / (inv_point[i] + total)
        for d in range(1, n_node):
            node_copy(d, b).wait_recv()
        pl.when(first_tm)(lambda: init_copy(b).wait())
        if n_tm > 1:
            pl.when(jnp.logical_not(first_tm))(lambda: prev_copy(b).wait_recv())
        for x in range(bricks):
            mine = [own[j, x, rows] for j in range(per)]
            states = [mine] + [[theirs[d - 1, j, x, rows] for j in range(per)] for d in range(1, n_node)]
            begin = start[x, rows]
            for i in range(per):
                q = mix[i][0][0] * states[0][0]
                for d in range(n_node):
                    for j in range(per):
                        if d or j:
                            q = q + mix[i][d][j] * states[d][j]
                even[i, x + 1, inside] = mine[i] + q
                rhs[i, x, rows] = (begin + q) * inv_point[i]

    def sweep(src, dst, b, last, planes):
        r = pl.multiple_of(b * ROWS, ROWS)
        rows = pl.ds(r, ROWS)
        inside = pl.ds(pl.multiple_of(r + PAD, 8), ROWS)
        for x in planes:
            xl, xr = fx[x, rows], fx[x + 1, rows]
            yl, yr = fyl[x, rows], fyr[x, rows]
            zl, zr = fzl[x, rows], fzr[x, rows]
            for i in range(per):
                window = src[i, x + 1, pl.ds(r, ROWS + 2 * PAD)]
                centre = window[PAD : PAD + ROWS]
                right = rhs[i, x, rows]
                value = xl * src[i, x, inside] + xr * src[i, x + 2, inside]
                value = value + yl * window[PAD - 1 : PAD - 1 + ROWS]
                value = value + yr * window[PAD + 1 : PAD + 1 + ROWS]
                value = value + zl * pltpu.roll(centre, 1, 1)
                value = value + zr * pltpu.roll(centre, width - 1, 1)
                value = (value + right) * inv[i, x, rows]
                if last:
                    out[0, i, x, rows] = value - (point[i] * right - start[x, rows])
                else:
                    dst[i, x + 1, inside] = value

    def receive(buffer, s, b):
        if n_space > 1:
            pl.when(has_lower)(lambda: halo_up(buffer, s, b).wait_recv())
            pl.when(has_upper)(lambda: halo_down(buffer, s, b).wait_recv())

    def send(buffer, s, b):
        if n_space > 1:
            @pl.when(has_upper)
            def _():
                pl.when(b > 0)(lambda: halo_up(buffer, s, b - 1).wait_send())
                halo_up(buffer, s, b).start()

            @pl.when(has_lower)
            def _():
                pl.when(b > 0)(lambda: halo_down(buffer, s, b - 1).wait_send())
                halo_down(buffer, s, b).start()

    def settle(buffer, s):
        if n_space > 1:
            pl.when(has_upper)(lambda: halo_up(buffer, s, chunks - 1).wait_send())
            pl.when(has_lower)(lambda: halo_down(buffer, s, chunks - 1).wait_send())

    def stage(src, dst, s, t, last=False):
        b = t - s

        @pl.when((b >= 0) & (b < chunks))
        def _():
            receive(src, s - 1, b)
            if last:
                sweep(src, dst, b, last, range(bricks))
            else:
                ends = sorted({0, bricks - 1})
                sweep(src, dst, b, last, ends)
                send(dst, s, b)
                sweep(src, dst, b, last, range(1, bricks - 1))

        if not last:
            pl.when(b == chunks)(lambda: settle(dst, s))

    @pl.loop(0, chunks + SWEEPS)
    def _(t):
        @pl.when(t < chunks)
        def _():
            first_stage(t)
            send(even, 0, t)

        pl.when(t == chunks)(lambda: settle(even, 0))

        @pl.loop(0, SWEEPS // 2 - 1)
        def _(j):
            stage(even, odd, 2 * j + 1, t)
            stage(odd, even, 2 * j + 2, t)

        stage(even, odd, SWEEPS - 1, t)
        stage(odd, None, SWEEPS, t, last=True)

    if n_space > 1:
        pl.when(has_upper)(lambda: k_up().wait_send())
        pl.when(has_lower)(lambda: k_down().wait_send())

    @pl.loop(0, chunks)
    def _(b):
        for d in range(1, n_node):
            node_copy(d, b).wait_send()
        if n_tm > 1:
            pl.when(jnp.logical_not(last_tm))(lambda: prev_copy(b).wait_send())


def body(n_node, n_tm, n_space, nodes, prev_final, u_init, conductivity):
    per, bricks, height, width = nodes.shape[1:]
    chunks = height // ROWS
    field = (bricks, height, width)
    f32 = jnp.float32
    vmem = pltpu.VMEM
    dma = pltpu.SemaphoreType.DMA
    others = max(n_node - 1, 1)
    return pl.pallas_call(
        functools.partial(kernel, (n_node, n_tm, n_space, per, bricks, height)),
        out_shape=pltpu.VMEM(nodes.shape, f32),
        in_specs=[pl.BlockSpec(memory_space=pltpu.HBM)] * 4,
        out_specs=pl.BlockSpec(memory_space=pltpu.VMEM),
        scratch_shapes=[
            vmem((per,) + field, f32),
            vmem((others, per) + field, f32),
            vmem(field, f32),
            vmem((per, bricks + 2, height + 2 * PAD, width), f32),
            vmem((per, bricks + 2, height + 2 * PAD, width), f32),
            vmem((bricks + 2, height + 2 * PAD, width), f32),
            vmem((bricks + 1, height, width), f32),
            vmem(field, f32),
            vmem(field, f32),
            vmem(field, f32),
            vmem(field, f32),
            vmem((per,) + field, f32),
            vmem((per,) + field, f32),
            dma((2,)),
            dma((2,)),
            dma((2,)),
            dma((others, chunks)),
            dma((others, chunks)),
            dma((chunks,)),
            dma((chunks,)),
            dma((2, SWEEPS)),
            dma((2, SWEEPS, chunks)),
        ],
        compiler_params=pltpu.CompilerParams(
            collective_id=0, has_side_effects=True, vmem_limit_bytes=48 * 1024 * 1024
        ),
        name="sdc_sweep",
    )(nodes, prev_final, u_init, conductivity)


def solution(mesh):
    in_specs = (
        P("tm", "node", "space", None, None),
        P("tm", "space", None, None),
        P("space", None, None),
        P("space", None, None),
    )
    out_specs = P("tm", "node", "space", None, None)
    sized = functools.partial(body, mesh.shape["node"], mesh.shape["tm"], mesh.shape["space"])
    return jax.shard_map(sized, mesh=mesh, in_specs=in_specs, out_specs=out_specs, check_vma=False)
```
